128 devices in a mesh: ty: 8 (over z, core), tx: 16 (over y, x).
Axes of the slice: x: 4, y: 4, z: 4, core: 2. Of those that a mesh axis runs over, the one named last changes fastest.
Arguments:
- strips: bfloat16 [2, 8, 16, 4, 8, 128, 128], P(None, 'ty', 'tx'), may hold values from -6 to 6
- centers: bfloat16 [2, 8, 16, 8, 128, 128], P(None, 'ty', 'tx'), may hold values from -6 to 6
- match_lists: int32 [2, 8, 16, 5, 8, 2], P(None, 'ty', 'tx'), may hold values from 0 to 1023, as said below
- match_counts: int32 [2, 8, 16, 5], P(None, 'ty', 'tx'), may hold values from 0 to 8, as said below
- spring_stiffness: float32 [2, 8, 16], P(None, 'ty', 'tx'), may hold values from 0.5 to 6
Outputs:
- vertex_shift: float32 [2, 2, 8, 16, 1024], P(None, None, 'ty', 'tx')
- match_shift: float32 [2, 2, 8, 16, 5, 8], P(None, None, 'ty', 'tx')
The draws below stay inside these ranges and needn't reach their ends.
Inputs may be any that keep to these rules, and one draw needn't show every extreme that they name: `match_lists`: entry [s, r, c, k, j, 0] is a vertex of tile (r, c) of section s and entry [s, r, c, k, j, 1] a vertex of its partner tile in direction k. The lists are mirrored: slot j of the east list of tile (r, c) equals slot j of the west list of tile (r, c+1) with its two vertices swapped; likewise south and north lists, and the cross lists of the two sections. `match_counts`: slots j below the count are matches, the others are unused. Counts are mirrored like the lists, and are 0 in directions that leave the slab.
All inputs are finite; a program needn't handle non-finite values.
Results may differ from the reference program's by a relative error of at most 0.0003.
Values may be sent and summed in bfloat16 or wider, within the bound.
No kernel may reach another device: no remote copies, remote signals or barrier semaphores. Data moves between devices by JAX's collectives and lax.ppermute only.
A program may use at most 128 MiB of HBM per device.

```python
import jax
import jax.numpy as jnp
from jax import lax

P_SIZE = 8
W = 128
V = 32
ITERS = 3
NTR = 8
NTC = 16


binomial_weights = (1.0, 6.0, 15.0, 20.0, 15.0, 6.0, 1.0)


unit_rescale = 4096.0 / 924.0


def smooth_field(field):
    for along in (-2, -1):
        total = jnp.zeros_like(field)
        for offset, factor in enumerate(binomial_weights):
            total = total + factor / 64.0 * jnp.roll(field, offset - 3, axis=along)
        field = total
    return field * unit_rescale


def texture(subkey, dims):
    base = jax.random.normal(subkey, dims, jnp.float32)
    return smooth_field(base)


def speckle(subkey, dims):
    return jax.random.normal(subkey, dims, jnp.float32)


def roll_patches(patches, offsets):

    def roll_single(patch, offset):
        return jnp.roll(jnp.roll(patch, offset[0], axis=0), offset[1], axis=1)
    flat = patches.reshape((-1, W, W))
    moved = jax.vmap(roll_single)(flat, offsets.reshape((-1, 2)))
    return moved.reshape(patches.shape)


def subpixel(patches, fractions):
    row_part = fractions[..., 0][..., None, None]
    col_part = fractions[..., 1][..., None, None]
    moved = (1.0 - row_part) * patches + row_part * jnp.roll(patches, 1, axis=-2)
    return (1.0 - col_part) * moved + col_part * jnp.roll(moved, 1, axis=-1)


def pixel_fields(key):
    subkeys = [jax.random.fold_in(key, 501 + number) for number in range(17)]
    edge_dims = (2, NTR, NTC, P_SIZE, W, W)
    largest_lag = W // 4
    east_tissue = texture(subkeys[0], edge_dims)
    south_tissue = texture(subkeys[1], edge_dims)
    cross_tissue = texture(subkeys[2], (NTR, NTC, P_SIZE, W, W))
    lags_east = jax.random.randint(subkeys[3], (2, NTR, NTC, P_SIZE, 2), -largest_lag, largest_lag + 1)
    lags_south = jax.random.randint(subkeys[4], (2, NTR, NTC, P_SIZE, 2), -largest_lag, largest_lag + 1)
    lags_cross = jax.random.randint(subkeys[5], (NTR, NTC, P_SIZE, 2), -largest_lag, largest_lag + 1)
    parts_east = jax.random.uniform(subkeys[14], (2, NTR, NTC, P_SIZE, 2), jnp.float32, 0.0, 1.0)
    parts_south = jax.random.uniform(subkeys[15], (2, NTR, NTC, P_SIZE, 2), jnp.float32, 0.0, 1.0)
    parts_cross = jax.random.uniform(subkeys[16], (NTR, NTC, P_SIZE, 2), jnp.float32, 0.0, 1.0)
    east_side = east_tissue + speckle(subkeys[6], edge_dims)
    west_moved = subpixel(roll_patches(east_tissue, lags_east), parts_east) + speckle(subkeys[7], edge_dims)
    west_side = jnp.concatenate([texture(subkeys[8], (2, NTR, 1, P_SIZE, W, W)), west_moved[:, :, :-1]], axis=2)
    south_side = south_tissue + speckle(subkeys[9], edge_dims)
    north_moved = subpixel(roll_patches(south_tissue, lags_south), parts_south) + speckle(subkeys[10], edge_dims)
    north_side = jnp.concatenate([texture(subkeys[11], (2, 1, NTC, P_SIZE, W, W)), north_moved[:, :-1]], axis=1)
    strips = jnp.stack([east_side, west_side, south_side, north_side], axis=3)
    first_center = cross_tissue + speckle(subkeys[12], (NTR, NTC, P_SIZE, W, W))
    second_center = subpixel(roll_patches(cross_tissue, lags_cross), parts_cross) + speckle(subkeys[13], (NTR, NTC, P_SIZE, W, W))
    centers = jnp.stack([first_center, second_center])
    return (jnp.clip(strips, -6.0, 6.0), jnp.clip(centers, -6.0, 6.0))


def draw_strips(key, part):
    return pixel_fields(key)[0].astype(jnp.bfloat16)


def draw_centers(key, part):
    return pixel_fields(key)[1].astype(jnp.bfloat16)


def match_graph(key):
    subkeys = [jax.random.fold_in(key, 901 + number) for number in range(14)]
    vertices = V * V
    edge_dims = (2, NTR, NTC, P_SIZE)
    own_east = jax.random.randint(subkeys[0], edge_dims, 0, vertices)
    far_east = jax.random.randint(subkeys[1], edge_dims, 0, vertices)
    own_south = jax.random.randint(subkeys[2], edge_dims, 0, vertices)
    far_south = jax.random.randint(subkeys[3], edge_dims, 0, vertices)
    own_cross = jax.random.randint(subkeys[4], (NTR, NTC, P_SIZE), 0, vertices)
    far_cross = jax.random.randint(subkeys[5], (NTR, NTC, P_SIZE), 0, vertices)
    spares = jax.random.randint(subkeys[6], (4, 2, NTR, NTC, P_SIZE), 0, vertices)
    west_own = jnp.concatenate([spares[0][:, :, :1], far_east[:, :, :-1]], axis=2)
    west_far = jnp.concatenate([spares[1][:, :, :1], own_east[:, :, :-1]], axis=2)
    north_own = jnp.concatenate([spares[2][:, :1], far_south[:, :-1]], axis=1)
    north_far = jnp.concatenate([spares[3][:, :1], own_south[:, :-1]], axis=1)
    cross_own = jnp.stack([own_cross, far_cross])
    cross_far = jnp.stack([far_cross, own_cross])
    owners = jnp.stack([own_east, west_own, own_south, north_own, cross_own], axis=3)
    partners = jnp.stack([far_east, west_far, far_south, north_far, cross_far], axis=3)
    lists = jnp.stack([owners, partners], axis=-1)
    columns = jnp.arange(NTC, dtype=jnp.int32)
    rows_index = jnp.arange(NTR, dtype=jnp.int32)
    count_east = jax.random.randint(subkeys[7], (2, NTR, NTC), 0, P_SIZE + 1)
    count_east = jnp.where(columns[None, None, :] == NTC - 1, 0, count_east)
    count_east = count_east.at[0, 0, 0].set(P_SIZE)
    count_west = jnp.concatenate([jnp.zeros((2, NTR, 1), jnp.int32), count_east[:, :, :-1]], axis=2)
    count_south = jax.random.randint(subkeys[8], (2, NTR, NTC), 0, P_SIZE + 1)
    count_south = jnp.where(rows_index[None, :, None] == NTR - 1, 0, count_south)
    count_north = jnp.concatenate([jnp.zeros((2, 1, NTC), jnp.int32), count_south[:, :-1]], axis=1)
    count_cross = jax.random.randint(subkeys[9], (NTR, NTC), 0, P_SIZE + 1)
    count_cross = jnp.stack([count_cross, count_cross])
    counts = jnp.stack([count_east, count_west, count_south, count_north, count_cross], axis=3)
    return (lists.astype(jnp.int32), counts.astype(jnp.int32))


def draw_match_lists(key, part):
    return match_graph(key)[0]


def draw_match_counts(key, part):
    return match_graph(key)[1]


def draw_spring_stiffness(key, part):
    tile_dims = (2, NTR, NTC)
    col_ramp = (jnp.arange(NTC, dtype=jnp.float32) / NTC)[None, None, :]
    subkey = jax.random.fold_in(key, 1301)
    base = jnp.exp(jax.random.uniform(subkey, tile_dims, jnp.float32, jnp.log(0.5), jnp.log(2.0)))
    result = base * jnp.power(2.8, col_ramp)
    return result.astype(jnp.float32)


def setup_inputs(seed: int = 0) -> dict:
    key_of = jax.random.split(jax.random.key(seed), 6)
    return {
        "strips": draw_strips(jax.random.fold_in(key_of[5], 71), 0),
        "centers": draw_centers(jax.random.fold_in(key_of[5], 71), 0),
        "match_lists": draw_match_lists(jax.random.fold_in(key_of[5], 71), 0),
        "match_counts": draw_match_counts(jax.random.fold_in(key_of[5], 71), 0),
        "spring_stiffness": draw_spring_stiffness(jax.random.fold_in(key_of[5], 71), 0),
    }


precise = lax.Precision.HIGHEST
anchor_weight = 0.05
epsilon = 1e-6


def lag_values():
    indices = jnp.arange(W, dtype=jnp.int32)
    midpoint = W // 2
    lagged = jnp.where(indices < midpoint, indices, jnp.where(indices == midpoint, 0, indices - W))
    return lagged.astype(jnp.float32)


def displacement(own_pixels, partner_pixels):
    own_spec = jnp.fft.fft2(own_pixels.astype(jnp.float32))
    partner_spec = jnp.fft.fft2(partner_pixels.astype(jnp.float32))
    surface = jnp.real(jnp.fft.ifft2(own_spec * jnp.conj(partner_spec))) / W
    squared = surface * surface
    weight = squared * squared
    totals = jnp.sum(weight, axis=(-2, -1)) + epsilon
    lagged = lag_values()
    toward_rows = jnp.sum(weight * lagged[:, None], axis=(-2, -1))
    toward_cols = jnp.sum(weight * lagged[None, :], axis=(-2, -1))
    return jnp.stack([toward_rows / totals, toward_cols / totals]) * (2.0 / W)


def neighbour_sum(vector):
    column = jnp.arange(V * V, dtype=jnp.int32) % V
    single = jnp.zeros(vector.shape[:-1] + (1,), vector.dtype)
    row_zeros = jnp.zeros(vector.shape[:-1] + (V,), vector.dtype)
    from_left = jnp.concatenate([single, vector[..., :-1]], axis=-1) * (column > 0).astype(vector.dtype)
    from_right = jnp.concatenate([vector[..., 1:], single], axis=-1) * (column < V - 1).astype(vector.dtype)
    from_above = jnp.concatenate([row_zeros, vector[..., :-V]], axis=-1)
    from_below = jnp.concatenate([vector[..., V:], row_zeros], axis=-1)
    return from_left + from_right + from_above + from_below


def reference(strips, centers, match_lists, match_counts, spring_stiffness):
    north_next = jnp.concatenate([strips[:, 1:, :, 3], jnp.zeros_like(strips[:, :1, :, 3])], axis=1)

    def row_shifts(row_index):
        tile_row = lax.dynamic_index_in_dim(strips, row_index, 1, keepdims=False)
        next_row = lax.dynamic_index_in_dim(north_next, row_index, 1, keepdims=False)
        middle = lax.dynamic_index_in_dim(centers, row_index, 1, keepdims=False)
        west_next = jnp.concatenate([tile_row[:, 1:, 1], jnp.zeros_like(tile_row[:, :1, 1])], axis=1)
        east_offset = displacement(tile_row[:, :, 0], west_next)
        south_offset = displacement(tile_row[:, :, 2], next_row)
        cross_offset = displacement(middle[0], middle[1])
        return east_offset, south_offset, cross_offset

    east_rows, south_rows, cross_rows = lax.map(row_shifts, jnp.arange(NTR, dtype=jnp.int32))
    shift_east = jnp.moveaxis(east_rows, 0, 2)
    shift_south = jnp.moveaxis(south_rows, 0, 2)
    cross = jnp.moveaxis(cross_rows, 0, 1)
    shift_west = jnp.concatenate([jnp.zeros_like(shift_east[:, :, :, :1]), -shift_east[:, :, :, :-1]], axis=3)
    shift_north = jnp.concatenate([jnp.zeros_like(shift_south[:, :, :1]), -shift_south[:, :, :-1]], axis=2)
    shift_cross = jnp.stack([cross, -cross], axis=1)
    match_shift = jnp.stack([shift_east, shift_west, shift_south, shift_north, shift_cross], axis=4)

    valid = (jnp.arange(P_SIZE, dtype=jnp.int32) < match_counts[..., None]).astype(jnp.float32)
    vertex_ids = jnp.arange(V * V, dtype=jnp.int32)
    own_table = (match_lists[..., 0, None] == vertex_ids).astype(jnp.float32) * valid[..., None]
    partner_table = (match_lists[..., 1, None] == vertex_ids).astype(jnp.float32)
    stiffness = spring_stiffness[..., None]
    degree = neighbour_sum(jnp.ones((V * V,), jnp.float32))
    diagonal = anchor_weight + stiffness * degree + jnp.sum(own_table, axis=(3, 4))
    rhs_values = jnp.einsum('strkjv,cstrkj->cstrv', own_table, match_shift, precision=precise)

    def apply_operator(vector):
        own_values = jnp.einsum('strkjv,cstrv->cstrkj', own_table, vector, precision=precise)
        beside = [
            jnp.concatenate([vector[:, :, :, 1:], jnp.zeros_like(vector[:, :, :, :1])], axis=3),
            jnp.concatenate([jnp.zeros_like(vector[:, :, :, :1]), vector[:, :, :, :-1]], axis=3),
            jnp.concatenate([vector[:, :, 1:], jnp.zeros_like(vector[:, :, :1])], axis=2),
            jnp.concatenate([jnp.zeros_like(vector[:, :, :1]), vector[:, :, :-1]], axis=2),
            vector[:, ::-1],
        ]
        partner_values = jnp.stack([jnp.einsum('strjv,cstrv->cstrj', partner_table[:, :, :, number], beside[number], precision=precise) for number in range(5)], axis=4)
        coupling = jnp.einsum('strkjv,cstrkj->cstrv', own_table, own_values - partner_values, precision=precise)
        return anchor_weight * vector + stiffness * (degree * vector - neighbour_sum(vector)) + coupling

    solution = jnp.zeros_like(rhs_values)
    residual = rhs_values
    precond = residual / diagonal
    direction = precond
    norm_now = jnp.sum(residual * precond)
    for iteration in range(ITERS):
        product = apply_operator(direction)
        step_size = norm_now / jnp.sum(direction * product)
        solution = solution + step_size * direction
        residual = residual - step_size * product
        precond = residual / diagonal
        norm_next = jnp.sum(residual * precond)
        direction = precond + (norm_next / norm_now) * direction
        norm_now = norm_next
    return solution, match_shift
```

```python
import functools

import jax
import jax.numpy as jnp
import numpy as np
from jax import lax
from jax.experimental import pallas as pl
from jax.experimental.pallas import tpu as pltpu
from jax.sharding import PartitionSpec as P

P_SIZE = 8
W = 128
V = 32
HALF = P_SIZE // 2
SLOTS = 5 * P_SIZE
U = 72

anchor_weight = 0.05
epsilon = 1e-06
f32 = jnp.float32
bf16 = jnp.bfloat16


def split_table(table):
    table = np.asarray(table, np.float32)
    high = table.astype(jnp.bfloat16)
    return high, (table - high.astype(np.float32)).astype(jnp.bfloat16)


def fourier_tables():
    idx = np.arange(W)
    angles = 2.0 * np.pi * ((idx[:, None] * idx[None, :]) % W) / W
    cos, sin = np.cos(angles), np.sin(angles)
    cos_h, cos_l = split_table(cos)
    sin_h, sin_l = split_table(sin)
    along_cols = np.concatenate(
        [np.concatenate([cos_h, sin_h], 1), np.concatenate([cos_l, sin_l], 1)], 0
    )
    half_cos, half_sin = np.zeros((U, W)), np.zeros((U, W))
    half_cos[: W // 2 + 1], half_sin[: W // 2 + 1] = cos[: W // 2 + 1], sin[: W // 2 + 1]
    along_rows = np.concatenate(
        [np.concatenate([half_cos, -half_sin], 1), np.concatenate([-half_sin, -half_cos], 1)], 0
    )
    along_rows = np.concatenate(split_table(along_rows), 0)
    back_cols = np.concatenate(
        [np.concatenate([cos, sin], 1), np.concatenate([-sin, cos], 1)], 0
    )
    back_cols = np.concatenate(split_table(back_cols), 0)
    back_rows = np.zeros((W, W))
    back_rows[:, 0] = 1.0
    back_rows[:, 1 : W // 2] = 2.0 * cos[:, 1 : W // 2]
    back_rows[:, W // 2] = cos[:, W // 2]
    back_rows[:, W // 2 + 1 :] = -2.0 * sin[:, 1 : W // 2]
    back_h, back_l = split_table(back_rows / float(W * W * W))
    back_rows = np.concatenate([back_h, back_h, back_l], 1)
    lag = np.where(idx < W // 2, idx, np.where(idx == W // 2, 0, idx - W)).astype(np.float32)
    lag_rows = np.broadcast_to(lag[:, None], (W, W)).copy()
    lag_cols = np.broadcast_to(lag[None, :], (P_SIZE, W)).copy()
    return along_cols, along_rows, back_cols, back_rows, lag_rows, lag_cols


def high_low(values):
    high = values.astype(bf16)
    return high, (values - high.astype(f32)).astype(bf16)


def dot(left, right):
    return jnp.dot(left, right, preferred_element_type=f32)


def correlate_two(own, partner, tables, high_ref, low_ref):
    along_cols, along_rows, back_cols, back_rows, lag_rows = tables
    spectra = []
    for side, patches in enumerate((own, partner)):
        for t, patch in enumerate(patches):
            high, low = high_low(dot(jnp.concatenate([patch, patch], 1), along_cols[...]))
            lanes = pl.ds(t * W, W)
            high_ref[side, 0:W, lanes] = high[:, :W]
            high_ref[side, W : 2 * W, lanes] = high[:, W:]
            low_ref[side, 0:W, lanes] = low[:, :W]
            low_ref[side, W : 2 * W, lanes] = low[:, W:]
        both = dot(along_rows[...], high_ref[side])
        spectra.append(
            both[: 2 * U] + both[2 * U :] + dot(along_rows[0 : 2 * U], low_ref[side])
        )
    own_re, own_im = spectra[0][:U], spectra[0][U:]
    par_re, par_im = spectra[1][:U], spectra[1][U:]
    cross_re = own_re * par_re + own_im * par_im
    cross_im = own_im * par_re - own_re * par_im
    cross = jnp.concatenate(
        [
            jnp.concatenate([cross_re[:, :W], cross_im[:, :W]], 1),
            jnp.concatenate([cross_re[:, W:], cross_im[:, W:]], 1),
        ],
        0,
    )
    high, low = high_low(cross)
    both = dot(jnp.concatenate([high, low], 0), back_cols[0 : 2 * W])
    partly = both[: 2 * U] + both[2 * U :] + dot(high, back_cols[2 * W : 4 * W])
    first = lax.broadcasted_iota(jnp.int32, (8, W), 0) == 0
    stacked = []
    for t in range(2):
        real, imag = partly[t * U : (t + 1) * U, :W], partly[t * U : (t + 1) * U, W:]
        top = jnp.where(first, real[W // 2 : W // 2 + 8], imag[0:8])
        stacked.append(jnp.concatenate([real[: W // 2], top, imag[8 : W // 2]], 0))
    high, low = high_low(jnp.concatenate(stacked, 1))
    surface = dot(back_rows[:, 0 : 2 * W], jnp.concatenate([high, low], 0)) + dot(
        back_rows[:, 2 * W : 3 * W], high
    )
    squared = surface * surface
    weight = squared * squared
    lagged = lag_rows[...]
    totals = jnp.sum(weight, axis=0, keepdims=True)
    rowwise = jnp.sum(weight * jnp.concatenate([lagged, lagged], 1), axis=0, keepdims=True)
    return totals, rowwise


def correlate_four(load_own, load_partner, tables, high_ref, low_ref, tot_ref, row_ref, base):
    for g in range(2):
        totals, rowwise = correlate_two(
            [load_own(2 * g), load_own(2 * g + 1)],
            [load_partner(2 * g), load_partner(2 * g + 1)],
            tables,
            high_ref.at[g],
            low_ref.at[g],
        )
        for t in range(2):
            tot_ref[pl.ds(base + 2 * g + t, 1), :] = totals[:, t * W : (t + 1) * W]
            row_ref[pl.ds(base + 2 * g + t, 1), :] = rowwise[:, t * W : (t + 1) * W]


def offsets_on_lanes(tot_ref, row_ref, lag_cols, targets):
    tot, row = tot_ref[...], row_ref[...]
    denominator = jnp.sum(tot, axis=1, keepdims=True) + epsilon
    toward_rows = jnp.sum(row, axis=1, keepdims=True)
    toward_cols = jnp.sum(tot * lag_cols[0:1, :], axis=1, keepdims=True)
    lane = lax.broadcasted_iota(jnp.int32, tot.shape, 1)
    rows = []
    for toward in (toward_rows, toward_cols):
        shift = toward / denominator * (2.0 / W)
        rows.append(
            jnp.sum(jnp.where(lane == targets, shift, 0.0), axis=0, keepdims=True)
        )
    return jnp.concatenate(rows + [jnp.zeros((6, W), f32)], 0)


def cross_kernel(own_ref, par_ref, t1, t2, t3, t4, t5, lag_cols, out_ref, high_ref, low_ref, tot_ref, row_ref):
    step = pl.program_id(0)
    correlate_four(
        lambda j: own_ref[0, 0, 0, j],
        lambda j: par_ref[0, 0, 0, j],
        (t1, t2, t3, t4, t5),
        high_ref,
        low_ref,
        tot_ref,
        row_ref,
        step * HALF,
    )

    @pl.when(step == 1)
    def _():
        targets = 4 * P_SIZE + lax.broadcasted_iota(jnp.int32, (P_SIZE, W), 0)
        offset = offsets_on_lanes(tot_ref, row_ref, lag_cols, targets)
        out_ref[...] = offset - pltpu.roll(offset, SLOTS, 1)


def edge_kernel(sides, own_ref, r0, r1, r2, r3, t1, t2, t3, t4, t5, lag_cols, out_ref, par_ref, high_ref, low_ref, tot_ref, row_ref):
    which, section = pl.program_id(0), pl.program_id(1)
    for number, ref in enumerate((r0, r1, r2, r3)):

        @pl.when(which == number)
        def _():
            par_ref[...] = ref[section]

    correlate_four(
        lambda j: own_ref[0, 0, 0, 0, j],
        lambda j: par_ref[j],
        (t1, t2, t3, t4, t5),
        high_ref,
        low_ref,
        tot_ref,
        row_ref,
        which * P_SIZE + section * HALF,
    )

    @pl.when((which == 3) & (section == 1))
    def _():
        pair = lax.broadcasted_iota(jnp.int32, (4 * P_SIZE, W), 0)
        start = jnp.zeros_like(pair)
        for number in range(4):
            side = sides[number]
            start = jnp.where(pair // P_SIZE == number, side * P_SIZE + (side % 2) * HALF, start)
        targets = start + (pair % P_SIZE) // HALF * SLOTS + pair % HALF
        out_ref[...] = offsets_on_lanes(tot_ref, row_ref, lag_cols, targets)


def corr_scratch(pairs):
    return [
        pltpu.VMEM((2, 2, 2 * W, 2 * W), bf16),
        pltpu.VMEM((2, 2, 2 * W, 2 * W), bf16),
        pltpu.VMEM((pairs, W), f32),
        pltpu.VMEM((pairs, W), f32),
    ]


def whole(array):
    return pl.BlockSpec(array.shape, lambda *_: (0,) * array.ndim)


def cross_offsets(centers, tables):
    return pl.pallas_call(
        cross_kernel,
        grid=(2,),
        in_specs=[
            pl.BlockSpec((1, 1, 1, HALF, W, W), lambda i: (0, 0, 0, i, 0, 0)),
            pl.BlockSpec((1, 1, 1, HALF, W, W), lambda i: (1, 0, 0, i, 0, 0)),
        ]
        + [whole(t) for t in tables],
        out_specs=pl.BlockSpec((8, W), lambda i: (0, 0)),
        out_shape=jax.ShapeDtypeStruct((8, W), f32),
        scratch_shapes=corr_scratch(P_SIZE),
        name="cross_corr",
    )(centers, centers, *tables)


def edge_offsets(sides, strips, received, tables):
    return pl.pallas_call(
        edge_kernel,
        grid_spec=pltpu.PrefetchScalarGridSpec(
            num_scalar_prefetch=1,
            grid=(4, 2),
            in_specs=[
                pl.BlockSpec(
                    (1, 1, 1, 1, HALF, W, W),
                    lambda i, s, sides: (s, 0, 0, sides[i], sides[i] % 2, 0, 0),
                )
            ]
            + [pl.BlockSpec(r.shape, lambda i, s, sides: (0, 0, 0, 0)) for r in received]
            + [pl.BlockSpec(t.shape, lambda i, s, sides: (0, 0)) for t in tables],
            out_specs=pl.BlockSpec((8, W), lambda i, s, sides: (0, 0)),
            scratch_shapes=[pltpu.VMEM((HALF, W, W), bf16)] + corr_scratch(4 * P_SIZE),
        ),
        out_shape=jax.ShapeDtypeStruct((8, W), f32),
        name="edge_corr",
    )(sides, strips, *received, *tables)


def three_terms(values):
    high = values.astype(bf16)
    rest = values - high.astype(f32)
    middle = rest.astype(bf16)
    return jnp.concatenate([high, middle, (rest - middle.astype(f32)).astype(bf16)], 0)


def slot_tables(slots):
    vertex = slots[0:1, :]
    hit = lax.broadcasted_iota(jnp.int32, (W, W), 0) == vertex % W
    row = lax.broadcasted_iota(jnp.int32, (32, W), 0)
    lane = lax.broadcasted_iota(jnp.int32, (32, W), 1)
    section = jnp.where(lane < SLOTS, 0, 1)
    inside = (row % 8 == vertex // W) & ((row // 8) % 2 == section) & (lane < 2 * SLOTS)
    return jnp.where(hit, 1.0, 0.0).astype(bf16), jnp.where(inside, 1.0, 0.0)


def gather(field, hit, inside):
    found = dot(three_terms(field), hit)
    found = (found[:32] + found[32:64] + found[64:]) * inside
    return (
        jnp.sum(found[:16], axis=0, keepdims=True),
        jnp.sum(found[16:], axis=0, keepdims=True),
    )


def scatter(values, hit, inside):
    spread = jnp.concatenate(
        [jnp.broadcast_to(values[0], (16, W)), jnp.broadcast_to(values[1], (16, W))], 0
    )
    placed = lax.dot_general(
        three_terms(spread * inside), hit, (((1,), (1,)), ((), ())), preferred_element_type=f32
    )
    return placed[:32] + placed[32:64] + placed[64:]


def neighbour_sum(field):
    row = lax.broadcasted_iota(jnp.int32, field.shape, 0) % 8
    lane = lax.broadcasted_iota(jnp.int32, field.shape, 1)
    total = jnp.where(lane % V > 0, pltpu.roll(field, 1, 1), 0.0)
    total = total + jnp.where(lane % V < V - 1, pltpu.roll(field, W - 1, 1), 0.0)
    above = pltpu.roll(field, V, 1)
    wrapped = jnp.where(row > 0, pltpu.roll(above, 1, 0), 0.0)
    total = total + jnp.where(lane >= V, above, wrapped)
    below = pltpu.roll(field, W - V, 1)
    wrapped = jnp.where(row < 7, pltpu.roll(below, field.shape[0] - 1, 0), 0.0)
    return total + jnp.where(lane < W - V, below, wrapped)


def stiffness_rows(stiffness):
    row = lax.broadcasted_iota(jnp.int32, (32, W), 0)
    return jnp.where((row // 8) % 2 == 0, stiffness[0], stiffness[1])


def sided(parity, messages):
    even_x, even_y = parity[0] == 0, parity[1] == 0
    p1, p2, p3, p4 = (m[0:2, :] for m in messages)
    east, west = jnp.where(even_x, p1, p2), jnp.where(even_x, p2, p1)
    south, north = jnp.where(even_y, p3, p4), jnp.where(even_y, p4, p3)
    return east, west, south, north


def lane_kinds(shape):
    lane = lax.broadcasted_iota(jnp.int32, shape, 1)
    within = jnp.where(lane < SLOTS, lane, lane - SLOTS)
    return lane, within // P_SIZE, within % P_SIZE


def to_partner(sides):
    east, west, south, north = sides
    _, kind, _ = lane_kinds((2, W))
    low = jnp.where(kind == 0, pltpu.roll(east, W - P_SIZE, 1), pltpu.roll(south, W - P_SIZE, 1))
    high = jnp.where(kind == 1, pltpu.roll(west, P_SIZE, 1), pltpu.roll(north, P_SIZE, 1))
    return jnp.where((kind == 0) | (kind == 2), low, high)


def partner_values(own, sides):
    lane, kind, _ = lane_kinds((2, W))
    crossed = jnp.where(
        lane < SLOTS, pltpu.roll(own, W - SLOTS, 1), pltpu.roll(own, SLOTS, 1)
    )
    return jnp.where(kind == 4, crossed, to_partner(sides))


def padded(rows):
    return jnp.concatenate([rows, jnp.zeros((6, W), f32)], 0)


def start_kernel(parity, stiffness, slots, valid, cross, edge, m1, m2, m3, m4, field_ref, vals_ref, shift_ref, inv_ref):
    _, kind, slot = lane_kinds((2, W))
    mirrored = to_partner(sided(parity, (m1, m2, m3, m4)))
    here = ((kind == 0) | (kind == 2)) == (slot < HALF)
    shift = jnp.where(kind == 4, cross[0:2, :], jnp.where(here, edge[0:2, :], -mirrored))
    shift_ref[...] = padded(shift)
    hit, inside = slot_tables(slots)
    live = valid[0:1, :]
    ones = jnp.ones((32, W), f32)
    counts = scatter((live, live), hit, inside)
    diagonal = anchor_weight + stiffness_rows(stiffness) * neighbour_sum(ones) + counts
    inverse = 1.0 / diagonal
    rhs = scatter((live * shift[0:1], live * shift[1:2]), hit, inside)
    field = rhs / diagonal
    field_ref[...] = field
    inv_ref[...] = inverse
    vals_ref[...] = padded(jnp.concatenate(gather(field, hit, inside), 0))


def advance(parity, stiffness, slots, valid, field, vals, messages, inverse):
    hit, inside = slot_tables(slots)
    live = valid[0:1, :]
    partner = partner_values(vals[0:2, :], sided(parity, messages)) * live
    springs = stiffness_rows(stiffness)
    coupled = scatter((partner[0:1], partner[1:2]), hit, inside)
    result = (springs * neighbour_sum(field[...]) + coupled) * inverse[...]
    return result, jnp.concatenate(gather(result, hit, inside), 0), springs


def step_kernel(parity, stiffness, slots, valid, inverse, field, vals, m1, m2, m3, m4, field_ref, vals_ref):
    result, found, _ = advance(
        parity, stiffness, slots, valid, field, vals, (m1, m2, m3, m4), inverse
    )
    field_ref[...] = result
    vals_ref[...] = padded(found)


def moments_kernel(parity, stiffness, slots, valid, inverse, first, field, vals, m1, m2, m3, m4, field_ref, send_ref):
    third, found, springs = advance(
        parity, stiffness, slots, valid, field, vals, (m1, m2, m3, m4), inverse
    )
    field_ref[...] = third
    w0, w1 = first[...], field[...]
    diagonal = 1.0 / inverse[...]
    products = [
        w0 * w0 * diagonal,
        w0 * w1 * diagonal,
        w1 * w1 * diagonal,
        w1 * third * diagonal,
        third * third * diagonal,
        third * springs * neighbour_sum(third),
    ]
    sums = jnp.concatenate(
        [jnp.sum(p, axis=0, keepdims=True) for p in products] + [jnp.zeros((2, W), f32)], 0
    )
    live = valid[0:1, :]
    found = found * live
    lane, kind, _ = lane_kinds((2, W))
    crossed = jnp.where((lane < SLOTS) & (kind == 4), found * pltpu.roll(found, W - SLOTS, 1), 0.0)
    row8 = lax.broadcasted_iota(jnp.int32, (8, W), 0)
    lane8 = lax.broadcasted_iota(jnp.int32, (8, W), 1)
    sums = sums + jnp.where(row8 == 5, 2.0 * jnp.sum(crossed, axis=0, keepdims=True), 0.0)
    moments = jnp.sum(
        jnp.where(lane8 == 2 * SLOTS + row8, jnp.sum(sums, axis=1, keepdims=True), 0.0),
        axis=0,
        keepdims=True,
    )
    forward = jnp.where(((kind == 0) | (kind == 2)) & (lane < 2 * SLOTS), found, 0.0)
    backward = jnp.where(((kind == 1) | (kind == 3)) & (lane < 2 * SLOTS), found, 0.0)
    sent = forward[0:1] + pltpu.roll(forward, P_SIZE, 1)[1:2] + moments
    answer = pltpu.roll(backward, W - P_SIZE, 1)[0:1] + backward[1:2]
    block = jnp.where(row8 % 2 == 0, sent, answer)
    for t in range(send_ref.shape[0] // 8):
        send_ref[t * 8 : (t + 1) * 8, :] = block


def finish_kernel(columns, gathered, first, second, third, out_ref):
    count = gathered.shape[0] // 2
    sent = gathered[pl.ds(0, count, stride=2), :]
    answer = gathered[pl.ds(1, count, stride=2), :]
    lane = lax.broadcasted_iota(jnp.int32, (count, W), 1)
    within = jnp.where(lane < SLOTS, lane, lane - SLOTS)
    facing = jnp.where(
        within < 2 * P_SIZE,
        pltpu.roll(answer, count - 1, 0),
        pltpu.roll(answer, count - columns, 0),
    )
    edges = jnp.where((within < 4 * P_SIZE) & (lane < 2 * SLOTS), sent * facing, 0.0)
    edges = 2.0 * jnp.sum(edges, axis=0, keepdims=True)
    totals = jnp.sum(sent, axis=0, keepdims=True)
    row8 = lax.broadcasted_iota(jnp.int32, (8, W), 0)
    lane8 = lax.broadcasted_iota(jnp.int32, (8, W), 1)
    picked = jnp.where(lane8 == 2 * SLOTS + row8, totals, 0.0) + jnp.where(row8 == 5, edges, 0.0)
    picked = jnp.sum(picked, axis=1, keepdims=True)
    nu = [picked[k : k + 1, :] for k in range(6)]

    def inner(p, q, shifted):
        total = jnp.zeros((1, 1), f32)
        for i, a in enumerate(p):
            for j, b in enumerate(q):
                moment = nu[i + j] - nu[i + j + 1] if shifted else nu[i + j]
                total = total + a * b * moment
        return total

    def add(p, q, factor):
        length = max(len(p), len(q))
        zero = jnp.zeros((1, 1), f32)
        p = p + [zero] * (length - len(p))
        q = q + [zero] * (length - len(q))
        return [a + factor * b for a, b in zip(p, q)]

    one = jnp.ones((1, 1), f32)
    residual, direction, solution = [one], [one], [jnp.zeros((1, 1), f32)]
    norm = inner(residual, residual, False)
    for iteration in range(3):
        step = norm / inner(direction, direction, True)
        solution = add(solution, direction, step)
        if iteration == 2:
            break
        moved = [-d for d in direction]
        image = add(direction + [jnp.zeros((1, 1), f32)], [jnp.zeros((1, 1), f32)] + moved, one)
        residual = add(residual, image, -step)
        latest = inner(residual, residual, False)
        direction = add(residual, direction, latest / norm)
        norm = latest
    out_ref[...] = solution[0] * first[...] + solution[1] * second[...] + solution[2] * third[...]


SMEM = pl.BlockSpec(memory_space=pltpu.SMEM)
VMEM = pl.BlockSpec(memory_space=pltpu.VMEM)


def shaped(*shapes):
    return [jax.ShapeDtypeStruct(s, f32) for s in shapes]


def local(columns, rows, strips, centers, match_lists, match_counts, spring_stiffness):
    tables = [jnp.asarray(t) for t in fourier_tables()]
    parity_x, parity_y = lax.axis_index("tx") % 2, lax.axis_index("ty") % 2
    parity = jnp.stack([parity_x, parity_y]).astype(jnp.int32)
    sides = jnp.stack([parity_x, 1 - parity_x, 2 + parity_y, 3 - parity_y]).astype(jnp.int32)

    def swaps(count, odd):
        pairs = [(i, i + 1) for i in range(odd, count - 1, 2)]
        return pairs + [(b, a) for a, b in pairs]

    routes = [
        ("tx", swaps(columns, 0)),
        ("tx", swaps(columns, 1)),
        ("ty", swaps(rows, 0)),
        ("ty", swaps(rows, 1)),
    ]

    def exchange(arrays):
        return [lax.ppermute(a, axis, route) for a, (axis, route) in zip(arrays, routes)]

    outgoing = []
    for number in range(4):
        side = sides[number]
        piece = lax.dynamic_slice(
            strips,
            (0, 0, 0, side, (1 - side % 2) * HALF, 0, 0),
            (2, 1, 1, 1, HALF, W, W),
        )
        outgoing.append(piece.reshape(2, HALF, W, W))
    received = exchange(outgoing)
    cross = cross_offsets(centers, tables)
    edge = edge_offsets(sides, strips, received, tables)

    def on_lanes(values):
        return jnp.pad(values.reshape(1, 2 * SLOTS), ((0, 7), (0, W - 2 * SLOTS)))

    slots = on_lanes(match_lists[..., 0])
    live = jnp.arange(P_SIZE, dtype=jnp.int32) < match_counts[..., None]
    valid = on_lanes(live.astype(f32))
    stiffness = spring_stiffness.reshape(2)

    messages = exchange([edge] * 4)
    first, vals, shift, inverse = pl.pallas_call(
        start_kernel,
        in_specs=[SMEM, SMEM] + [VMEM] * 8,
        out_specs=[VMEM] * 4,
        out_shape=shaped((32, W), (8, W), (8, W), (32, W)),
        name="start",
    )(parity, stiffness, slots, valid, cross, edge, *messages)
    messages = exchange([vals] * 4)
    second, vals = pl.pallas_call(
        step_kernel,
        in_specs=[SMEM, SMEM] + [VMEM] * 9,
        out_specs=[VMEM] * 2,
        out_shape=shaped((32, W), (8, W)),
        name="step",
    )(parity, stiffness, slots, valid, inverse, first, vals, *messages)
    messages = exchange([vals] * 4)
    third, sent = pl.pallas_call(
        moments_kernel,
        in_specs=[SMEM, SMEM] + [VMEM] * 10,
        out_specs=[VMEM] * 2,
        out_shape=shaped((32, W), (2 * rows * columns, W)),
        name="moments",
    )(parity, stiffness, slots, valid, inverse, first, second, vals, *messages)
    gathered = lax.all_to_all(sent, ("ty", "tx"), 0, 0, tiled=True)
    solution = pl.pallas_call(
        functools.partial(finish_kernel, columns),
        in_specs=[VMEM] * 4,
        out_specs=VMEM,
        out_shape=jax.ShapeDtypeStruct((32, W), f32),
        name="finish",
    )(gathered, first, second, third)
    vertex_shift = solution.reshape(2, 2, 1, 1, V * V)
    match_shift = shift[0:2, 0 : 2 * SLOTS].reshape(2, 2, 1, 1, 5, P_SIZE)
    return vertex_shift, match_shift


def solution(mesh):
    return jax.shard_map(
        functools.partial(local, mesh.shape["tx"], mesh.shape["ty"]),
        mesh=mesh,
        in_specs=(
            P(None, "ty", "tx", None, None, None, None),
            P(None, "ty", "tx", None, None, None),
            P(None, "ty", "tx", None, None, None),
            P(None, "ty", "tx", None),
            P(None, "ty", "tx"),
        ),
        out_specs=(P(None, None, "ty", "tx", None), P(None, None, "ty", "tx", None, None)),
        check_vma=False,
    )
```

```python
import functools

import jax
import jax.numpy as jnp
import numpy as np
from jax import lax
from jax.experimental import pallas as pl
from jax.experimental.pallas import tpu as pltpu
from jax.sharding import PartitionSpec as P

P_SIZE = 8
W = 128
V = 32
HALF = P_SIZE // 2
SLOTS = 5 * P_SIZE
U = 72

anchor_weight = 0.05
epsilon = 1e-06
f32 = jnp.float32
bf16 = jnp.bfloat16
SMEM = pl.BlockSpec(memory_space=pltpu.SMEM)
VMEM = pl.BlockSpec(memory_space=pltpu.VMEM)
CORR_VMEM = 16 * 2**20
SMALL = pltpu.CompilerParams(vmem_limit_bytes=2 * 2**20)


def split_table(table):
    table = np.asarray(table, np.float32)
    high = table.astype(jnp.bfloat16)
    return high, (table - high.astype(np.float32)).astype(jnp.bfloat16)


def fourier_tables():
    idx = np.arange(W)
    angles = 2.0 * np.pi * ((idx[:, None] * idx[None, :]) % W) / W
    cos, sin = np.cos(angles), np.sin(angles)
    cos_h, cos_l = split_table(cos)
    sin_h, sin_l = split_table(sin)
    along_cols = np.concatenate(
        [np.concatenate([cos_h, sin_h], 1), np.concatenate([cos_l, sin_l], 1)], 0
    )
    half_cos, half_sin = np.zeros((U, W)), np.zeros((U, W))
    half_cos[: W // 2 + 1], half_sin[: W // 2 + 1] = cos[: W // 2 + 1], sin[: W // 2 + 1]
    along_rows = np.concatenate(
        [np.concatenate([half_cos, -half_sin], 1), np.concatenate([-half_sin, -half_cos], 1)], 0
    )
    along_rows = np.concatenate(split_table(along_rows), 0)
    back_cols = np.concatenate(
        [np.concatenate([cos, sin], 1), np.concatenate([-sin, cos], 1)], 0
    )
    back_cols = np.concatenate(split_table(back_cols), 0)
    back_rows = np.zeros((W, W))
    back_rows[:, 0] = 1.0
    back_rows[:, 1 : W // 2] = 2.0 * cos[:, 1 : W // 2]
    back_rows[:, W // 2] = cos[:, W // 2]
    back_rows[:, W // 2 + 1 :] = -2.0 * sin[:, 1 : W // 2]
    back_h, back_l = split_table(back_rows / float(W * W * W))
    back_rows = np.concatenate([back_h, back_h, back_l], 1)
    lag = np.where(idx < W // 2, idx, np.where(idx == W // 2, 0, idx - W)).astype(np.float32)
    lag_rows = np.broadcast_to(lag[:, None], (W, W)).copy()
    lag_cols = np.broadcast_to(lag[None, :], (P_SIZE, W)).copy()
    return along_cols, along_rows, back_cols, back_rows, lag_rows, lag_cols


def high_low(values):
    high = values.astype(bf16)
    return high, (values - high.astype(f32)).astype(bf16)


def dot(left, right):
    return jnp.dot(left, right, preferred_element_type=f32)


def correlate(own, partner, tables, high_ref, low_ref, tot_ref, row_ref):
    along_cols, along_rows, back_cols, back_rows, lag_rows = tables
    groups = P_SIZE // 2
    for side, patches in enumerate((own, partner)):
        high, low = high_low(dot(jnp.concatenate([patches, patches], 1), along_cols[...]))
        for j in range(P_SIZE):
            g, lanes = j // 2, pl.ds(j % 2 * W, W)
            for ref, part in ((high_ref, high), (low_ref, low)):
                ref[g, side, 0:W, lanes] = part[j * W : (j + 1) * W, :W]
                ref[g, side, W : 2 * W, lanes] = part[j * W : (j + 1) * W, W:]
    highs, lows = [], []
    for g in range(groups):
        spectra = []
        for side in range(2):
            both = dot(along_rows[...], high_ref[g, side])
            spectra.append(
                both[: 2 * U] + both[2 * U :] + dot(along_rows[0 : 2 * U], low_ref[g, side])
            )
        own_re, own_im = spectra[0][:U], spectra[0][U:]
        par_re, par_im = spectra[1][:U], spectra[1][U:]
        cross_re = own_re * par_re + own_im * par_im
        cross_im = own_im * par_re - own_re * par_im
        cross = jnp.concatenate(
            [
                jnp.concatenate([cross_re[:, :W], cross_im[:, :W]], 1),
                jnp.concatenate([cross_re[:, W:], cross_im[:, W:]], 1),
            ],
            0,
        )
        high, low = high_low(cross)
        highs.append(high)
        lows.append(low)
    count = 2 * U * groups
    both = dot(jnp.concatenate(highs + lows, 0), back_cols[0 : 2 * W])
    partly = both[:count] + both[count:]
    partly = partly + dot(jnp.concatenate(highs, 0), back_cols[2 * W : 4 * W])
    first = lax.broadcasted_iota(jnp.int32, (8, W), 0) == 0
    lagged = lag_rows[...]
    lagged = jnp.concatenate([lagged, lagged], 1)
    for g in range(groups):
        stacked = []
        for t in range(2):
            piece = partly[(2 * g + t) * U : (2 * g + t + 1) * U]
            real, imag = piece[:, :W], piece[:, W:]
            top = jnp.where(first, real[W // 2 : W // 2 + 8], imag[0:8])
            stacked.append(jnp.concatenate([real[: W // 2], top, imag[8 : W // 2]], 0))
        high, low = high_low(jnp.concatenate(stacked, 1))
        surface = dot(back_rows[:, 0 : 2 * W], jnp.concatenate([high, low], 0)) + dot(
            back_rows[:, 2 * W : 3 * W], high
        )
        squared = surface * surface
        weight = squared * squared
        totals = jnp.sum(weight, axis=0, keepdims=True)
        rowwise = jnp.sum(weight * lagged, axis=0, keepdims=True)
        for t in range(2):
            tot_ref[pl.ds(2 * g + t, 1), :] = totals[:, t * W : (t + 1) * W]
            row_ref[pl.ds(2 * g + t, 1), :] = rowwise[:, t * W : (t + 1) * W]


def offsets_on_lanes(tot_ref, row_ref, lag_cols, targets):
    tot, row = tot_ref[...], row_ref[...]
    denominator = jnp.sum(tot, axis=1, keepdims=True) + epsilon
    toward_rows = jnp.sum(row, axis=1, keepdims=True)
    toward_cols = jnp.sum(tot * lag_cols[0:1, :], axis=1, keepdims=True)
    lane = lax.broadcasted_iota(jnp.int32, tot.shape, 1)
    rows = []
    for toward in (toward_rows, toward_cols):
        shift = toward / denominator * (2.0 / W)
        rows.append(
            jnp.sum(jnp.where(lane == targets, shift, 0.0), axis=0, keepdims=True)
        )
    return jnp.concatenate(rows + [jnp.zeros((6, W), f32)], 0)


def cross_kernel(pixels, t1, t2, t3, t4, t5, lag_cols, out_ref, high_ref, low_ref, tot_ref, row_ref):
    correlate(
        pixels[0, 0, 0].reshape(P_SIZE * W, W),
        pixels[1, 0, 0].reshape(P_SIZE * W, W),
        (t1, t2, t3, t4, t5),
        high_ref,
        low_ref,
        tot_ref,
        row_ref,
    )
    targets = 4 * P_SIZE + lax.broadcasted_iota(jnp.int32, (P_SIZE, W), 0)
    offset = offsets_on_lanes(tot_ref, row_ref, lag_cols, targets)
    out_ref[...] = offset - pltpu.roll(offset, SLOTS, 1)


def side_of(number):
    place = lax.axis_index("tx" if number < 2 else "ty")
    return 2 * (number // 2) + lax.rem(place + number, 2)


def edge_kernel(number, strips, received, t1, t2, t3, t4, t5, lag_cols, out_ref, high_ref, low_ref, tot_ref, row_ref):
    side = side_of(number)
    start = lax.rem(side, 2) * HALF
    correlate(
        strips[:, 0, 0, side, pl.ds(start, HALF)].reshape(P_SIZE * W, W),
        received[...].reshape(P_SIZE * W, W),
        (t1, t2, t3, t4, t5),
        high_ref,
        low_ref,
        tot_ref,
        row_ref,
    )
    pair = lax.broadcasted_iota(jnp.int32, (P_SIZE, W), 0)
    targets = side * P_SIZE + start + pair // HALF * SLOTS + pair % HALF
    out_ref[...] = offsets_on_lanes(tot_ref, row_ref, lag_cols, targets)


def corr_call(kernel, name, *args):
    return pl.pallas_call(
        kernel,
        in_specs=[VMEM] * len(args),
        out_specs=VMEM,
        out_shape=jax.ShapeDtypeStruct((8, W), f32),
        scratch_shapes=[
            pltpu.VMEM((P_SIZE // 2, 2, 2 * W, 2 * W), bf16),
            pltpu.VMEM((P_SIZE // 2, 2, 2 * W, 2 * W), bf16),
            pltpu.VMEM((P_SIZE, W), f32),
            pltpu.VMEM((P_SIZE, W), f32),
        ],
        compiler_params=pltpu.CompilerParams(vmem_limit_bytes=CORR_VMEM),
        name=name,
    )(*args)


def three_terms(values):
    high = values.astype(bf16)
    rest = values - high.astype(f32)
    middle = rest.astype(bf16)
    return jnp.concatenate([high, middle, (rest - middle.astype(f32)).astype(bf16)], 0)


def slot_tables(slots):
    vertex = slots[0:1, :]
    hit = lax.broadcasted_iota(jnp.int32, (W, W), 0) == vertex % W
    row = lax.broadcasted_iota(jnp.int32, (32, W), 0)
    lane = lax.broadcasted_iota(jnp.int32, (32, W), 1)
    section = jnp.where(lane < SLOTS, 0, 1)
    inside = (row % 8 == vertex // W) & ((row // 8) % 2 == section) & (lane < 2 * SLOTS)
    return jnp.where(hit, 1.0, 0.0).astype(bf16), jnp.where(inside, 1.0, 0.0)


def gather(field, hit, inside):
    found = dot(three_terms(field), hit)
    found = (found[:32] + found[32:64] + found[64:]) * inside
    return (
        jnp.sum(found[:16], axis=0, keepdims=True),
        jnp.sum(found[16:], axis=0, keepdims=True),
    )


def scatter(values, hit, inside):
    spread = jnp.concatenate(
        [jnp.broadcast_to(values[0], (16, W)), jnp.broadcast_to(values[1], (16, W))], 0
    )
    placed = lax.dot_general(
        three_terms(spread * inside), hit, (((1,), (1,)), ((), ())), preferred_element_type=f32
    )
    return placed[:32] + placed[32:64] + placed[64:]


def neighbour_sum(field):
    row = lax.broadcasted_iota(jnp.int32, field.shape, 0) % 8
    lane = lax.broadcasted_iota(jnp.int32, field.shape, 1)
    total = jnp.where(lane % V > 0, pltpu.roll(field, 1, 1), 0.0)
    total = total + jnp.where(lane % V < V - 1, pltpu.roll(field, W - 1, 1), 0.0)
    above = pltpu.roll(field, V, 1)
    wrapped = jnp.where(row > 0, pltpu.roll(above, 1, 0), 0.0)
    total = total + jnp.where(lane >= V, above, wrapped)
    below = pltpu.roll(field, W - V, 1)
    wrapped = jnp.where(row < 7, pltpu.roll(below, field.shape[0] - 1, 0), 0.0)
    return total + jnp.where(lane < W - V, below, wrapped)


def stiffness_rows(stiffness):
    row = lax.broadcasted_iota(jnp.int32, (32, W), 0)
    return jnp.where((row // 8) % 2 == 0, stiffness[0, 0, 0], stiffness[1, 0, 0])


def sided(messages):
    even_x, even_y = lax.rem(lax.axis_index("tx"), 2) == 0, lax.rem(lax.axis_index("ty"), 2) == 0
    p1, p2, p3, p4 = (m[0:2, :] for m in messages)
    east, west = jnp.where(even_x, p1, p2), jnp.where(even_x, p2, p1)
    south, north = jnp.where(even_y, p3, p4), jnp.where(even_y, p4, p3)
    return east, west, south, north


def lane_kinds(shape):
    lane = lax.broadcasted_iota(jnp.int32, shape, 1)
    within = jnp.where(lane < SLOTS, lane, lane - SLOTS)
    return lane, within // P_SIZE, within % P_SIZE


def to_partner(sides):
    east, west, south, north = sides
    _, kind, _ = lane_kinds((2, W))
    low = jnp.where(kind == 0, pltpu.roll(east, W - P_SIZE, 1), pltpu.roll(south, W - P_SIZE, 1))
    high = jnp.where(kind == 1, pltpu.roll(west, P_SIZE, 1), pltpu.roll(north, P_SIZE, 1))
    return jnp.where((kind == 0) | (kind == 2), low, high)


def partner_values(own, sides):
    lane, kind, _ = lane_kinds((2, W))
    crossed = jnp.where(
        lane < SLOTS, pltpu.roll(own, W - SLOTS, 1), pltpu.roll(own, SLOTS, 1)
    )
    return jnp.where(kind == 4, crossed, to_partner(sides))


def padded(rows):
    return jnp.concatenate([rows, jnp.zeros((6, W), f32)], 0)


def prepare_kernel(stiffness, counts, lists, slots_ref, valid_ref, inv_ref):
    slots_ref[...] = jnp.zeros((8, W), jnp.int32)
    lane = lax.broadcasted_iota(jnp.int32, (8, W), 1)
    used = jnp.zeros((8, W), jnp.int32)
    for section in range(2):
        for kind in range(5):
            place = section * SLOTS + kind * P_SIZE
            slots_ref[0:1, place : place + P_SIZE] = lists[section, 0, 0, kind, 0:1, :]
            here = (lane >= place) & (lane < place + P_SIZE)
            used = jnp.where(here, place + counts[section, 0, 0, kind], used)
    live = jnp.where(lane < used, 1.0, 0.0)
    valid_ref[...] = live
    hit, inside = slot_tables(slots_ref)
    numbers = scatter((live[0:1], live[0:1]), hit, inside)
    springs = stiffness_rows(stiffness) * neighbour_sum(jnp.ones((32, W), f32))
    inv_ref[...] = 1.0 / (anchor_weight + springs + numbers)


def start_kernel(columns, rows, slots, valid, inverse, cross, e1, e2, e3, e4, m1, m2, m3, m4, field_ref, vals_ref, shift_ref):
    _, kind, slot = lane_kinds((2, W))
    mirrored = to_partner(sided((m1, m2, m3, m4)))
    edge = e1[0:2, :] + e2[0:2, :] + e3[0:2, :] + e4[0:2, :]
    here = ((kind == 0) | (kind == 2)) == (slot < HALF)
    shift = jnp.where(kind == 4, cross[0:2, :], jnp.where(here, edge, -mirrored))
    tx, ty = lax.axis_index("tx"), lax.axis_index("ty")
    closed = (kind == 0) & (tx == columns - 1) | (kind == 1) & (tx == 0)
    closed = closed | (kind == 2) & (ty == rows - 1) | (kind == 3) & (ty == 0)
    shift = jnp.where(closed, 0.0, shift)
    shift_ref[...] = padded(shift)
    hit, inside = slot_tables(slots)
    live = valid[0:1, :]
    field = scatter((live * shift[0:1], live * shift[1:2]), hit, inside) * inverse[...]
    field_ref[...] = field
    vals_ref[...] = padded(jnp.concatenate(gather(field, hit, inside), 0))


def advance(stiffness, slots, valid, field, vals, messages, inverse):
    hit, inside = slot_tables(slots)
    live = valid[0:1, :]
    partner = partner_values(vals[0:2, :], sided(messages)) * live
    springs = stiffness_rows(stiffness)
    coupled = scatter((partner[0:1], partner[1:2]), hit, inside)
    result = (springs * neighbour_sum(field[...]) + coupled) * inverse[...]
    return result, jnp.concatenate(gather(result, hit, inside), 0), springs


def step_kernel(stiffness, slots, valid, inverse, field, vals, m1, m2, m3, m4, field_ref, vals_ref):
    result, found, _ = advance(
        stiffness, slots, valid, field, vals, (m1, m2, m3, m4), inverse
    )
    field_ref[...] = result
    vals_ref[...] = padded(found)


def moments_kernel(stiffness, slots, valid, inverse, first, field, vals, m1, m2, m3, m4, field_ref, send_ref):
    third, found, springs = advance(
        stiffness, slots, valid, field, vals, (m1, m2, m3, m4), inverse
    )
    field_ref[...] = third
    w0, w1 = first[...], field[...]
    diagonal = 1.0 / inverse[...]
    products = [
        w0 * w0 * diagonal,
        w0 * w1 * diagonal,
        w1 * w1 * diagonal,
        w1 * third * diagonal,
        third * third * diagonal,
        third * springs * neighbour_sum(third),
    ]
    sums = jnp.concatenate(
        [jnp.sum(p, axis=0, keepdims=True) for p in products] + [jnp.zeros((2, W), f32)], 0
    )
    live = valid[0:1, :]
    found = found * live
    lane, kind, _ = lane_kinds((2, W))
    crossed = jnp.where((lane < SLOTS) & (kind == 4), found * pltpu.roll(found, W - SLOTS, 1), 0.0)
    row8 = lax.broadcasted_iota(jnp.int32, (8, W), 0)
    lane8 = lax.broadcasted_iota(jnp.int32, (8, W), 1)
    sums = sums + jnp.where(row8 == 5, 2.0 * jnp.sum(crossed, axis=0, keepdims=True), 0.0)
    moments = jnp.sum(
        jnp.where(lane8 == 2 * SLOTS + row8, jnp.sum(sums, axis=1, keepdims=True), 0.0),
        axis=0,
        keepdims=True,
    )
    forward = jnp.where(((kind == 0) | (kind == 2)) & (lane < 2 * SLOTS), found, 0.0)
    backward = jnp.where(((kind == 1) | (kind == 3)) & (lane < 2 * SLOTS), found, 0.0)
    sent = forward[0:1] + pltpu.roll(forward, P_SIZE, 1)[1:2] + moments
    answer = pltpu.roll(backward, W - P_SIZE, 1)[0:1] + backward[1:2]
    block = jnp.where(row8 % 2 == 0, sent, answer)
    for t in range(send_ref.shape[0] // 8):
        send_ref[t * 8 : (t + 1) * 8, :] = block


def finish_kernel(columns, gathered, first, second, third, out_ref):
    count = gathered.shape[0] // 2
    sent = gathered[pl.ds(0, count, stride=2), :]
    answer = gathered[pl.ds(1, count, stride=2), :]
    lane = lax.broadcasted_iota(jnp.int32, (count, W), 1)
    within = jnp.where(lane < SLOTS, lane, lane - SLOTS)
    facing = jnp.where(
        within < 2 * P_SIZE,
        pltpu.roll(answer, count - 1, 0),
        pltpu.roll(answer, count - columns, 0),
    )
    edges = jnp.where((within < 4 * P_SIZE) & (lane < 2 * SLOTS), sent * facing, 0.0)
    edges = 2.0 * jnp.sum(edges, axis=0, keepdims=True)
    totals = jnp.sum(sent, axis=0, keepdims=True)
    row8 = lax.broadcasted_iota(jnp.int32, (8, W), 0)
    lane8 = lax.broadcasted_iota(jnp.int32, (8, W), 1)
    picked = jnp.where(lane8 == 2 * SLOTS + row8, totals, 0.0) + jnp.where(row8 == 5, edges, 0.0)
    picked = jnp.sum(picked, axis=1, keepdims=True)
    nu = [picked[k : k + 1, :] for k in range(6)]

    def inner(p, q, shifted):
        total = jnp.zeros((1, 1), f32)
        for i, a in enumerate(p):
            for j, b in enumerate(q):
                moment = nu[i + j] - nu[i + j + 1] if shifted else nu[i + j]
                total = total + a * b * moment
        return total

    def add(p, q, factor):
        length = max(len(p), len(q))
        zero = jnp.zeros((1, 1), f32)
        p = p + [zero] * (length - len(p))
        q = q + [zero] * (length - len(q))
        return [a + factor * b for a, b in zip(p, q)]

    one = jnp.ones((1, 1), f32)
    residual, direction, solution = [one], [one], [jnp.zeros((1, 1), f32)]
    norm = inner(residual, residual, False)
    for iteration in range(3):
        step = norm / inner(direction, direction, True)
        solution = add(solution, direction, step)
        if iteration == 2:
            break
        moved = [-d for d in direction]
        image = add(direction + [jnp.zeros((1, 1), f32)], [jnp.zeros((1, 1), f32)] + moved, one)
        residual = add(residual, image, -step)
        latest = inner(residual, residual, False)
        direction = add(residual, direction, latest / norm)
        norm = latest
    out_ref[...] = solution[0] * first[...] + solution[1] * second[...] + solution[2] * third[...]


def shaped(*shapes):
    return [jax.ShapeDtypeStruct(s, f32) for s in shapes]


def local(columns, rows, strips, centers, match_lists, match_counts, spring_stiffness):
    tables = [jnp.asarray(t) for t in fourier_tables()]

    def swaps(count, odd):
        pairs = [(i, (i + 1) % count) for i in range(odd, count, 2)]
        return pairs + [(b, a) for a, b in pairs]

    routes = [
        ("tx", swaps(columns, 0)),
        ("tx", swaps(columns, 1)),
        ("ty", swaps(rows, 0)),
        ("ty", swaps(rows, 1)),
    ]

    def exchange(array, number):
        return lax.ppermute(array, *routes[number])

    received = []
    for number in range(4):
        side = side_of(number)
        piece = lax.dynamic_slice(
            strips,
            (0, 0, 0, side, (1 - lax.rem(side, 2)) * HALF, 0, 0),
            (2, 1, 1, 1, HALF, W, W),
        )
        received.append(exchange(piece.reshape(2, HALF, W, W), number))
    slots, valid, inverse = pl.pallas_call(
        prepare_kernel,
        in_specs=[SMEM, SMEM, VMEM],
        out_specs=[VMEM] * 3,
        out_shape=[jax.ShapeDtypeStruct((8, W), jnp.int32)] + shaped((8, W), (32, W)),
        compiler_params=SMALL,
        name="prepare",
    )(spring_stiffness, match_counts, jnp.swapaxes(match_lists, 4, 5))
    edges, messages = [None] * 4, [None] * 4
    for number in (2, 3, 0, 1):
        edges[number] = corr_call(
            functools.partial(edge_kernel, number),
            f"edge_{number}",
            strips,
            received[number],
            *tables,
        )
        messages[number] = exchange(edges[number], number)
    cross = corr_call(cross_kernel, "cross", centers, *tables)
    first, vals, shift = pl.pallas_call(
        functools.partial(start_kernel, columns, rows),
        in_specs=[VMEM] * 12,
        out_specs=[VMEM] * 3,
        out_shape=shaped((32, W), (8, W), (8, W)),
        compiler_params=SMALL,
        name="start",
    )(slots, valid, inverse, cross, *edges, *messages)
    messages = [exchange(vals, number) for number in range(4)]
    second, vals = pl.pallas_call(
        step_kernel,
        in_specs=[SMEM] + [VMEM] * 9,
        out_specs=[VMEM] * 2,
        out_shape=shaped((32, W), (8, W)),
        compiler_params=SMALL,
        name="step",
    )(spring_stiffness, slots, valid, inverse, first, vals, *messages)
    messages = [exchange(vals, number) for number in range(4)]
    third, sent = pl.pallas_call(
        moments_kernel,
        in_specs=[SMEM] + [VMEM] * 10,
        out_specs=[VMEM] * 2,
        out_shape=shaped((32, W), (2 * rows * columns, W)),
        compiler_params=SMALL,
        name="moments",
    )(spring_stiffness, slots, valid, inverse, first, second, vals, *messages)
    gathered = lax.all_to_all(sent, ("ty", "tx"), 0, 0, tiled=True)
    solution = pl.pallas_call(
        functools.partial(finish_kernel, columns),
        in_specs=[VMEM] * 4,
        out_specs=VMEM,
        out_shape=jax.ShapeDtypeStruct((32, W), f32),
        compiler_params=SMALL,
        name="finish",
    )(gathered, first, second, third)
    vertex_shift = solution.reshape(2, 2, 1, 1, V * V)
    match_shift = shift[0:2, 0 : 2 * SLOTS].reshape(2, 2, 1, 1, 5, P_SIZE)
    return vertex_shift, match_shift


def solution(mesh):
    return jax.shard_map(
        functools.partial(local, mesh.shape["tx"], mesh.shape["ty"]),
        mesh=mesh,
        in_specs=(
            P(None, "ty", "tx", None, None, None, None),
            P(None, "ty", "tx", None, None, None),
            P(None, "ty", "tx", None, None, None),
            P(None, "ty", "tx", None),
            P(None, "ty", "tx"),
        ),
        out_specs=(P(None, None, "ty", "tx", None), P(None, None, "ty", "tx", None, None)),
        check_vma=False,
    )
```
